512 devices in a mesh: dp: 32 (over x, y), seq: 16 (over z, core).
Axes of the slice: x: 4, y: 8, z: 8, core: 2. Of those that a mesh axis runs over, the one named last changes fastest.
Arguments:
- residual_stream: bfloat16 [262144, 2048], P(('dp', 'seq')), parts along dimension 0, may hold values from -6 to 6
- octet_readout: bfloat16 [256, 2048], replicated, may hold values from -6 to 6
- downsampling_filter: bfloat16 [32, 256, 96], replicated, may hold values from -0.375 to 0.375
- sharpness_factor: float32 [8], replicated, may hold values from 4 to 20
- widening_filter: bfloat16 [32, 32, 256], replicated, may hold values from -2 to 2
Outputs:
- logits: bfloat16 [262144, 256], P(('dp', 'seq')), parts along dimension 0
The draws below stay inside these ranges and needn't reach their ends.
There are 32 independent parts, one for each index of `dp`. The reference program is written for one: setup_inputs(seed, part) draws one part's arguments, and reference() takes and returns one part's arrays. A program takes and returns all parts, laid end to end along the dimension named above; an argument that names none is the same for every part. Nothing has to cross between parts.
All inputs are finite; a program needn't handle non-finite values.
Results may differ from the reference program's by a relative error of at most 0.0052.
Values may be sent and summed in bfloat16 or wider, within the bound.
A program may use at most 64 MiB of HBM per device.

```python
import math
import jax
import jax.numpy as jnp
from jax import lax

D = 2048
GROUPS = 32
SECTION_HALF_ATT = 8
HEAD_DIM = 128
VOCAB = 256
SHORTEN = 4
DG = 64
OG = 32
BYTES = 8192
TOKENS = 2048


def steps_of(own_key, dims, cuts, smallest, high):
    loudness, own = 1.0, jax.random.fold_in(own_key, 6)
    for dim, blocks in cuts:
        heights = jnp.exp(jax.random.uniform(jax.random.fold_in(own, dim), (blocks,), jnp.float32, smallest / len(cuts), high / len(cuts)))
        loudness = loudness * jnp.repeat(heights, dims[dim] // blocks).reshape([-1 if axis == dim else 1 for axis in range(len(dims))])
    return loudness


def noise(key, extent, scale, reach, split=(), kind=jnp.bfloat16):
    result = jax.random.normal(key, extent, jnp.float32) * scale
    if len(split) > 0:
        result = steps_of(key, extent, split, -0.22, 0.18) * result
    return jnp.clip(result, min=-reach, max=reach).astype(kind)


def setup_inputs(seed: int = 0, part: int = 0) -> dict:
    arg_keys = jax.random.split(jax.random.key(seed), 6)
    part_splits = jax.random.split(jax.random.fold_in(arg_keys[5], part), 6)
    residual_stream = noise(part_splits[0], (BYTES, D), 1.0, 6.0, ((0, 16),))
    octet_readout = noise(arg_keys[1], (VOCAB, D), 1.0, 6.0)
    downsampling_filter = noise(arg_keys[2], (GROUPS, SHORTEN * DG, 3 * OG), (SHORTEN * DG) ** -0.5, 0.375)
    sharpness_factor = jnp.clip(jnp.exp(jax.random.uniform(arg_keys[3], (SECTION_HALF_ATT,), jnp.float32, math.log(4.0), math.log(20.0))), 4.0, 20.0)
    widening_filter = noise(arg_keys[4], (GROUPS, OG, SHORTEN * DG), 8 ** -0.5, 2.0)
    return {"residual_stream": residual_stream, "octet_readout": octet_readout, "downsampling_filter": downsampling_filter, "sharpness_factor": sharpness_factor, "widening_filter": widening_filter}


def normalize(vectors):
    return vectors * lax.rsqrt(lax.optimization_barrier(jnp.sum(vectors * vectors, axis=-1, keepdims=True)) + 1e-06)

def reference(residual_stream, octet_readout, downsampling_filter, sharpness_factor, widening_filter):
    shifted = jnp.concatenate([jnp.zeros((SHORTEN - 1, D), jnp.bfloat16), residual_stream[:BYTES - SHORTEN + 1]], 0)
    windows = shifted.reshape(TOKENS, SHORTEN, GROUPS, DG).astype(jnp.float32)
    kernel = downsampling_filter.reshape(GROUPS, SHORTEN, DG, 3 * OG).astype(jnp.float32)
    mixed_out = jnp.einsum('jtgc,gtco->jgo', windows, kernel)
    queries = normalize(mixed_out[:, :, :OG].reshape(TOKENS, SECTION_HALF_ATT, HEAD_DIM)).astype(jnp.bfloat16)
    key_unit = normalize(mixed_out[:, :, OG:2 * OG].reshape(TOKENS, SECTION_HALF_ATT, HEAD_DIM)).astype(jnp.bfloat16)
    values = mixed_out[:, :, 2 * OG:].reshape(TOKENS, SECTION_HALF_ATT, HEAD_DIM).astype(jnp.bfloat16)
    queries = lax.optimization_barrier(queries)
    lookup_real_vector = lax.optimization_barrier(key_unit).astype(jnp.float32)
    value_float = lax.optimization_barrier(values).astype(jnp.float32)
    block_size = math.gcd(TOKENS, 512)
    key_pos = jnp.arange(TOKENS, dtype=jnp.int32)
    sharpness_vertical = sharpness_factor[:, None, None]

    def one_block(block_index):
        asking_tile = lax.dynamic_slice_in_dim(queries, block_index * block_size, block_size, 0).astype(jnp.float32)
        similarity_matrix = jnp.einsum('jsg,isg->sji', asking_tile, lookup_real_vector) * sharpness_vertical
        query_pos = block_index * block_size + jnp.arange(block_size, dtype=jnp.int32)
        future_masked = key_pos[None, :] <= query_pos[:, None]
        softmax_shares = jnp.where(future_masked[None], jnp.exp(similarity_matrix - sharpness_vertical), jnp.zeros((), jnp.float32))
        denom_sum = lax.optimization_barrier(jnp.sum(softmax_shares, axis=-1))
        weights_low = lax.optimization_barrier(softmax_shares.astype(jnp.bfloat16)).astype(jnp.float32)
        weighted = jnp.einsum('hqk,khd->qhd', weights_low, value_float)
        return (weighted / jnp.transpose(denom_sum)[:, :, None]).astype(jnp.bfloat16)
    attended = lax.map(one_block, jnp.arange(TOKENS // block_size, dtype=jnp.int32))
    attended = attended.reshape(TOKENS, GROUPS, OG).astype(jnp.float32)
    upsampled = jnp.einsum('jgc,gcu->jgu', attended, widening_filter.astype(jnp.float32))
    upsampled = upsampled.reshape(TOKENS, GROUPS, SHORTEN, DG).transpose(0, 2, 1, 3).reshape(BYTES, D)
    hidden = residual_stream.astype(jnp.float32) + upsampled
    normed = (hidden * lax.rsqrt(lax.optimization_barrier(jnp.mean(hidden * hidden, axis=-1, keepdims=True)) + 1e-05)).astype(jnp.bfloat16)
    logits = jnp.dot(normed, octet_readout.T, preferred_element_type=jnp.float32) * D ** (-0.5)
    return logits.astype(jnp.bfloat16)
```

```python
import jax
import jax.numpy as jnp
from jax import lax
from jax.sharding import PartitionSpec as P

SHORTEN = 4


def shifted_2(array, axis, by):
    count = lax.axis_size(axis)
    pairs = [(i, i + by) for i in range(count) if 0 <= i + by < count]
    return lax.ppermute(array, axis, pairs)


def passed_along(block, axis, distance):
    devices = range(lax.axis_size(axis))
    route = [((i - distance) % len(devices), i) for i in devices]
    return lax.ppermute(block, axis, route)


def normalize(vectors):
    return vectors * lax.rsqrt(jnp.sum(vectors * vectors, axis=-1, keepdims=True) + 1e-06)


def shorten(shifted, kernel_part, groups):
    byte_rows, model_width = shifted.shape
    windows = shifted.reshape(byte_rows // SHORTEN, SHORTEN, groups, model_width // groups)
    kernel = kernel_part.reshape(groups, SHORTEN, model_width // groups, kernel_part.shape[2])
    return jnp.einsum("jtgc,gtco->jgo", windows, kernel, preferred_element_type=jnp.float32)


def on_device(
    residual_stream, octet_readout, downsampling_filter, sharpness_factor, widening_filter
):
    byte_rows = residual_stream.shape[0]
    model_width = residual_stream.shape[1]
    groups = downsampling_filter.shape[0]
    group_width = model_width // groups
    per_group = downsampling_filter.shape[2] // 3
    attention_number = sharpness_factor.shape[0]
    head_size = groups * per_group // attention_number
    tokens_here = byte_rows // SHORTEN
    rim_rows = SHORTEN - 1
    left_rim = shifted_2(residual_stream[byte_rows - rim_rows :], "seq", 1)
    shifted = jnp.concatenate([left_rim, residual_stream[: byte_rows - rim_rows]], 0)
    mixed_out = shorten(shifted, downsampling_filter, groups)
    queries = normalize(
        mixed_out[:, :, :per_group].reshape(tokens_here, attention_number, head_size)
    ).astype(jnp.bfloat16)
    key_unit = normalize(
        mixed_out[:, :, per_group : 2 * per_group].reshape(tokens_here, attention_number, head_size)
    ).astype(jnp.bfloat16)
    values = (
        mixed_out[:, :, 2 * per_group :]
        .reshape(tokens_here, attention_number, head_size)
        .astype(jnp.bfloat16)
    )
    my_index = lax.axis_index("seq")
    first_token = my_index * tokens_here
    sharpness_vertical = sharpness_factor[:, None, None]
    query_pos = first_token + jnp.arange(tokens_here, dtype=jnp.int32)

    stacked = jnp.stack([key_unit, values], 0)
    gathered = lax.all_gather(stacked, "seq", axis=1, tiled=True)
    all_keys, all_values = gathered[0], gathered[1]
    similarity_matrix = (
        jnp.einsum("jsg,isg->sji", queries, all_keys, preferred_element_type=jnp.float32)
        * sharpness_vertical
    )
    key_pos = jnp.arange(all_keys.shape[0], dtype=jnp.int32)
    future_masked = key_pos[None, :] <= query_pos[:, None]
    softmax_shares = jnp.where(
        future_masked[None],
        jnp.exp(similarity_matrix - sharpness_vertical),
        jnp.zeros((), jnp.float32),
    )
    denom_sum = jnp.sum(softmax_shares, axis=-1)
    weighted = jnp.einsum(
        "hqk,khd->qhd",
        softmax_shares.astype(jnp.bfloat16),
        all_values,
        preferred_element_type=jnp.float32,
    )
    attended = (weighted / jnp.transpose(denom_sum)[:, :, None]).astype(jnp.bfloat16)
    attended = attended.reshape(tokens_here, groups, per_group)
    upsampled = jnp.einsum(
        "jgc,gcu->jgu", attended, widening_filter, preferred_element_type=jnp.float32
    )
    upsampled = (
        upsampled.reshape(tokens_here, groups, SHORTEN, group_width)
        .transpose(0, 2, 1, 3)
        .reshape(byte_rows, model_width)
    )
    hidden = residual_stream.astype(jnp.float32) + upsampled
    normed = (hidden * lax.rsqrt(jnp.mean(hidden * hidden, axis=-1, keepdims=True) + 1e-05)).astype(
        jnp.bfloat16
    )
    logits = lax.dot_general(
        normed, octet_readout, (((1,), (1,)), ((), ())), preferred_element_type=jnp.float32
    ) * model_width ** (-0.5)
    return logits.astype(jnp.bfloat16)


def solution(mesh):
    in_specs = (P(("dp", "seq"), None), P(), P(), P(), P())
    out_specs = P(("dp", "seq"), None)
    return jax.shard_map(
        on_device, mesh=mesh, in_specs=in_specs, out_specs=out_specs, check_vma=False
    )
```

```python
import jax
import jax.numpy as jnp
from jax import lax
from jax.experimental import pallas as pl
from jax.experimental.pallas import tpu as pltpu
from jax.sharding import PartitionSpec as P

SHORTEN = 4


def shifted_2(array, axis, by):
    count = lax.axis_size(axis)
    pairs = [(i, i + by) for i in range(count) if 0 <= i + by < count]
    return lax.ppermute(array, axis, pairs)


def normalize(vectors):
    return vectors * lax.rsqrt(jnp.sum(vectors * vectors, axis=-1, keepdims=True) + 1e-06)


def shorten(shifted, kernel_part, groups):
    byte_rows, model_width = shifted.shape
    windows = shifted.reshape(byte_rows // SHORTEN, SHORTEN, groups, model_width // groups)
    kernel = kernel_part.reshape(groups, SHORTEN, model_width // groups, kernel_part.shape[2])
    return jnp.einsum("jtgc,gtco->jgo", windows, kernel, preferred_element_type=jnp.float32)


def widening_blocks(widening_filter, heads):
    groups, per_group, span = widening_filter.shape
    gph = groups // heads
    width = span // SHORTEN
    wf = widening_filter.reshape(heads, gph, per_group, SHORTEN, width)
    wf = wf.transpose(3, 0, 1, 2, 4)[:, :, :, :, None, :]
    eye = jnp.eye(gph, dtype=jnp.bool_)[:, None, :, None]
    blocks = jnp.where(eye, wf, jnp.zeros((), wf.dtype))
    return blocks.reshape(SHORTEN, heads, gph * per_group, gph * width)


def post_kernel(idx_ref, sharp_ref, q_ref, kv_ref, wup_ref, res_ref, oct_ref, out_ref, att_scr):
    me = idx_ref[0]
    heads, tq, hd = q_ref.shape
    f32, bf16 = jnp.float32, jnp.bfloat16
    qpos = me * tq + lax.broadcasted_iota(jnp.int32, (tq, tq), 0)
    kio = lax.broadcasted_iota(jnp.int32, (tq, tq), 1)
    for h in range(heads):
        q = q_ref[h]
        sharp = sharp_ref[h]

        def body(d, carry, q=q, sharp=sharp, h=h):
            num, den = carry
            s = lax.dot_general(
                q, kv_ref[0, d, h], (((1,), (1,)), ((), ())), preferred_element_type=f32
            ) * sharp
            w = jnp.where(d * tq + kio <= qpos, jnp.exp(s - sharp), jnp.zeros((), f32))
            den = den + jnp.sum(w, axis=1, keepdims=True)
            num = num + jnp.dot(w.astype(bf16), kv_ref[1, d, h], preferred_element_type=f32)
            return num, den

        num, den = lax.fori_loop(
            0, me + 1, body, (jnp.zeros((tq, hd), f32), jnp.zeros((tq, 1), f32))
        )
        att_scr[:, h * hd : (h + 1) * hd] = (num / den).astype(bf16)

    rows, width = res_ref.shape
    row_blocks = rows // 128
    tok_blk = 128 // SHORTEN
    n_chunks = wup_ref.shape[1]
    cin = wup_ref.shape[2]
    cout = wup_ref.shape[3]
    r_i = lax.broadcasted_iota(jnp.int32, (128, tok_blk), 0)
    j_i = lax.broadcasted_iota(jnp.int32, (128, tok_blk), 1)
    for rb in range(row_blocks):
        a_blk = att_scr[pl.ds(rb * tok_blk, tok_blk), :]
        expanded = []
        for t in range(SHORTEN):
            sel = (r_i == SHORTEN * j_i + t).astype(bf16)
            expanded.append(jnp.dot(sel, a_blk, preferred_element_type=f32).astype(bf16))
        hid = []
        ss = jnp.zeros((128, 1), f32)
        for k in range(n_chunks):
            u = jnp.dot(expanded[0][:, k * cin : (k + 1) * cin], wup_ref[0, k], preferred_element_type=f32)
            for t in range(1, SHORTEN):
                u = u + jnp.dot(
                    expanded[t][:, k * cin : (k + 1) * cin], wup_ref[t, k], preferred_element_type=f32
                )
            hcol = res_ref[pl.ds(rb * 128, 128), pl.ds(k * cout, cout)].astype(f32) + u
            hid.append(hcol)
            ss = ss + jnp.sum(hcol * hcol, axis=1, keepdims=True)
        scale = lax.rsqrt(ss / width + 1e-05)
        acc = None
        for k in range(n_chunks):
            part = lax.dot_general(
                (hid[k] * scale).astype(bf16),
                oct_ref[:, pl.ds(k * cout, cout)],
                (((1,), (1,)), ((), ())),
                preferred_element_type=f32,
            )
            acc = part if acc is None else acc + part
        out_ref[pl.ds(rb * 128, 128), :] = (acc * width ** (-0.5)).astype(out_ref.dtype)


def on_device(
    residual_stream, octet_readout, downsampling_filter, sharpness_factor, widening_filter
):
    byte_rows = residual_stream.shape[0]
    model_width = residual_stream.shape[1]
    groups = downsampling_filter.shape[0]
    per_group = downsampling_filter.shape[2] // 3
    attention_number = sharpness_factor.shape[0]
    head_size = groups * per_group // attention_number
    tokens_here = byte_rows // SHORTEN
    rim_rows = SHORTEN - 1
    left_rim = shifted_2(residual_stream[byte_rows - rim_rows :], "seq", 1)
    shifted = jnp.concatenate([left_rim, residual_stream[: byte_rows - rim_rows]], 0)
    mixed_out = shorten(shifted, downsampling_filter, groups)

    def heads_first(x):
        return x.reshape(tokens_here, attention_number, head_size).transpose(1, 0, 2)

    queries = heads_first(normalize(
        mixed_out[:, :, :per_group].reshape(tokens_here, attention_number, head_size)
    ).astype(jnp.bfloat16))
    key_unit = heads_first(normalize(
        mixed_out[:, :, per_group : 2 * per_group].reshape(tokens_here, attention_number, head_size)
    ).astype(jnp.bfloat16))
    values = heads_first(mixed_out[:, :, 2 * per_group :].astype(jnp.bfloat16))
    stacked = jnp.stack([key_unit, values], 0)[:, None]
    gathered = lax.all_gather(stacked, "seq", axis=1, tiled=True)
    my_index = lax.axis_index("seq").astype(jnp.int32).reshape(1)
    wup = widening_blocks(widening_filter, attention_number)
    vmem = pl.BlockSpec(memory_space=pltpu.VMEM)
    smem = pl.BlockSpec(memory_space=pltpu.SMEM)
    return pl.pallas_call(
        post_kernel,
        out_shape=jax.ShapeDtypeStruct((byte_rows, octet_readout.shape[0]), jnp.bfloat16),
        in_specs=[smem, smem, vmem, vmem, vmem, vmem, vmem],
        out_specs=vmem,
        scratch_shapes=[pltpu.VMEM((tokens_here, attention_number * head_size), jnp.bfloat16)],
        compiler_params=pltpu.CompilerParams(vmem_limit_bytes=60 * 1024 * 1024),
    )(my_index, sharpness_factor, queries, gathered, wup, residual_stream, octet_readout)


def solution(mesh):
    in_specs = (P(("dp", "seq"), None), P(), P(), P(), P())
    out_specs = P(("dp", "seq"), None)
    return jax.shard_map(
        on_device, mesh=mesh, in_specs=in_specs, out_specs=out_specs, check_vma=False
    )
```

```python
import jax
import jax.numpy as jnp
from jax import lax
from jax.experimental import pallas as pl
from jax.experimental.pallas import tpu as pltpu
from jax.sharding import PartitionSpec as P

SHORTEN = 4


def shifted_2(array, axis, by):
    count = lax.axis_size(axis)
    pairs = [(i, i + by) for i in range(count) if 0 <= i + by < count]
    return lax.ppermute(array, axis, pairs)


def normalize(vectors):
    return vectors * lax.rsqrt(jnp.sum(vectors * vectors, axis=-1, keepdims=True) + 1e-06)


def widening_blocks(widening_filter, heads):
    groups, per_group, span = widening_filter.shape
    gph = groups // heads
    width = span // SHORTEN
    wf = widening_filter.reshape(heads, gph, per_group, SHORTEN, width)
    wf = wf.transpose(3, 0, 1, 2, 4)[:, :, :, :, None, :]
    eye = jnp.eye(gph, dtype=jnp.bool_)[:, None, :, None]
    blocks = jnp.where(eye, wf, jnp.zeros((), wf.dtype))
    return blocks.reshape(SHORTEN, heads, gph * per_group, gph * width)


def shortening_blocks(downsampling_filter, heads):
    groups, span, outs = downsampling_filter.shape
    gph = groups // heads
    width = span // SHORTEN
    per_group = outs // 3
    w = downsampling_filter.reshape(heads, gph, SHORTEN, width, 3, per_group)
    w = w.transpose(2, 0, 1, 3, 4, 5)[:, :, :, :, :, None, :]
    eye = jnp.eye(gph, dtype=jnp.bool_)[:, None, None, :, None]
    blocks = jnp.where(eye, w, jnp.zeros((), w.dtype))
    return blocks.reshape(SHORTEN, heads, gph * width, 3 * gph * per_group)


def shorten_kernel(res_ref, rim_ref, wd_ref, q_ref, kv_ref):
    f32, bf16 = jnp.float32, jnp.bfloat16
    rows = res_ref.shape[0]
    tokens = rows // SHORTEN
    heads = wd_ref.shape[1]
    cin = wd_ref.shape[2]
    hd = wd_ref.shape[3] // 3
    j_i = lax.broadcasted_iota(jnp.int32, (tokens, rows), 0)
    r_i = lax.broadcasted_iota(jnp.int32, (tokens, rows), 1)
    first = lax.broadcasted_iota(jnp.int32, (tokens, 1), 0) == 0
    res = res_ref[...]
    picked = []
    for t in range(SHORTEN):
        sel = (r_i == SHORTEN * j_i + t - (SHORTEN - 1)).astype(bf16)
        x = jnp.dot(sel, res, preferred_element_type=f32).astype(bf16)
        if t < SHORTEN - 1:
            x = jnp.where(first, rim_ref[pl.ds(t, 1), :], x)
        picked.append(x)
    for k in range(heads):
        acc = None
        for t in range(SHORTEN):
            part = jnp.dot(picked[t][:, k * cin : (k + 1) * cin], wd_ref[t, k], preferred_element_type=f32)
            acc = part if acc is None else acc + part
        q = acc[:, :hd]
        key = acc[:, hd : 2 * hd]
        q_ref[k] = normalize(q).astype(bf16)
        kv_ref[0, 0, k] = normalize(key).astype(bf16)
        kv_ref[1, 0, k] = acc[:, 2 * hd :].astype(bf16)


def post_kernel(idx_ref, sharp_ref, q_ref, kv_ref, wup_ref, res_ref, oct_ref, out_ref, att_scr):
    me = idx_ref[0]
    heads, tq, hd = q_ref.shape
    f32, bf16 = jnp.float32, jnp.bfloat16
    qpos = me * tq + lax.broadcasted_iota(jnp.int32, (tq, tq), 0)
    kio = lax.broadcasted_iota(jnp.int32, (tq, tq), 1)
    for h in range(heads):
        q = q_ref[h]
        sharp = sharp_ref[h]

        def body(d, carry, q=q, sharp=sharp, h=h):
            num, den = carry
            s = lax.dot_general(
                q, kv_ref[0, d, h], (((1,), (1,)), ((), ())), preferred_element_type=f32
            ) * sharp
            w = jnp.where(d * tq + kio <= qpos, jnp.exp(s - sharp), jnp.zeros((), f32))
            den = den + jnp.sum(w, axis=1, keepdims=True)
            num = num + jnp.dot(w.astype(bf16), kv_ref[1, d, h], preferred_element_type=f32)
            return num, den

        num, den = lax.fori_loop(
            0, me + 1, body, (jnp.zeros((tq, hd), f32), jnp.zeros((tq, 1), f32))
        )
        att_scr[:, h * hd : (h + 1) * hd] = (num / den).astype(bf16)

    rows, width = res_ref.shape
    row_blocks = rows // 128
    tok_blk = 128 // SHORTEN
    n_chunks = wup_ref.shape[1]
    cin = wup_ref.shape[2]
    cout = wup_ref.shape[3]
    r_i = lax.broadcasted_iota(jnp.int32, (128, tok_blk), 0)
    j_i = lax.broadcasted_iota(jnp.int32, (128, tok_blk), 1)
    for rb in range(row_blocks):
        a_blk = att_scr[pl.ds(rb * tok_blk, tok_blk), :]
        expanded = []
        for t in range(SHORTEN):
            sel = (r_i == SHORTEN * j_i + t).astype(bf16)
            expanded.append(jnp.dot(sel, a_blk, preferred_element_type=f32).astype(bf16))
        hid = []
        ss = jnp.zeros((128, 1), f32)
        for k in range(n_chunks):
            u = jnp.dot(expanded[0][:, k * cin : (k + 1) * cin], wup_ref[0, k], preferred_element_type=f32)
            for t in range(1, SHORTEN):
                u = u + jnp.dot(
                    expanded[t][:, k * cin : (k + 1) * cin], wup_ref[t, k], preferred_element_type=f32
                )
            hcol = res_ref[pl.ds(rb * 128, 128), pl.ds(k * cout, cout)].astype(f32) + u
            hid.append(hcol)
            ss = ss + jnp.sum(hcol * hcol, axis=1, keepdims=True)
        scale = lax.rsqrt(ss / width + 1e-05)
        acc = None
        for k in range(n_chunks):
            part = lax.dot_general(
                (hid[k] * scale).astype(bf16),
                oct_ref[:, pl.ds(k * cout, cout)],
                (((1,), (1,)), ((), ())),
                preferred_element_type=f32,
            )
            acc = part if acc is None else acc + part
        out_ref[pl.ds(rb * 128, 128), :] = (acc * width ** (-0.5)).astype(out_ref.dtype)


def on_device(
    residual_stream, octet_readout, downsampling_filter, sharpness_factor, widening_filter
):
    byte_rows = residual_stream.shape[0]
    groups = downsampling_filter.shape[0]
    per_group = downsampling_filter.shape[2] // 3
    attention_number = sharpness_factor.shape[0]
    head_size = groups * per_group // attention_number
    tokens_here = byte_rows // SHORTEN
    rim_rows = SHORTEN - 1
    left_rim = shifted_2(residual_stream[byte_rows - rim_rows :], "seq", 1)
    wd = shortening_blocks(downsampling_filter, attention_number)
    vmem = pl.BlockSpec(memory_space=pltpu.VMEM)
    smem = pl.BlockSpec(memory_space=pltpu.SMEM)
    queries, stacked = pl.pallas_call(
        shorten_kernel,
        out_shape=(
            jax.ShapeDtypeStruct((attention_number, tokens_here, head_size), jnp.bfloat16),
            jax.ShapeDtypeStruct((2, 1, attention_number, tokens_here, head_size), jnp.bfloat16),
        ),
        in_specs=[vmem, vmem, vmem],
        out_specs=(vmem, vmem),
        compiler_params=pltpu.CompilerParams(vmem_limit_bytes=60 * 1024 * 1024),
    )(residual_stream, left_rim, wd)
    gathered = lax.all_gather(stacked, "seq", axis=1, tiled=True)
    my_index = lax.axis_index("seq").astype(jnp.int32).reshape(1)
    wup = widening_blocks(widening_filter, attention_number)
    return pl.pallas_call(
        post_kernel,
        out_shape=jax.ShapeDtypeStruct((byte_rows, octet_readout.shape[0]), jnp.bfloat16),
        in_specs=[smem, smem, vmem, vmem, vmem, vmem, vmem],
        out_specs=vmem,
        scratch_shapes=[pltpu.VMEM((tokens_here, attention_number * head_size), jnp.bfloat16)],
        compiler_params=pltpu.CompilerParams(vmem_limit_bytes=60 * 1024 * 1024),
    )(my_index, sharpness_factor, queries, gathered, wup, residual_stream, octet_readout)


def solution(mesh):
    in_specs = (P(("dp", "seq"), None), P(), P(), P(), P())
    out_specs = P(("dp", "seq"), None)
    return jax.shard_map(
        on_device, mesh=mesh, in_specs=in_specs, out_specs=out_specs, check_vma=False
    )
```

```python
import jax
import jax.numpy as jnp
from jax import lax
from jax.experimental import pallas as pl
from jax.experimental.pallas import tpu as pltpu
from jax.sharding import PartitionSpec as P

SHORTEN = 4


def shifted_2(array, axis, by):
    count = lax.axis_size(axis)
    pairs = [(i, i + by) for i in range(count) if 0 <= i + by < count]
    return lax.ppermute(array, axis, pairs)


def normalize(vectors):
    return vectors * lax.rsqrt(jnp.sum(vectors * vectors, axis=-1, keepdims=True) + 1e-06)


def widening_blocks(widening_filter, heads):
    groups, per_group, span = widening_filter.shape
    gph = groups // heads
    width = span // SHORTEN
    wf = widening_filter.reshape(heads, gph, per_group, SHORTEN, width)
    wf = wf.transpose(3, 0, 1, 2, 4)[:, :, :, :, None, :]
    eye = jnp.eye(gph, dtype=jnp.bool_)[:, None, :, None]
    blocks = jnp.where(eye, wf, jnp.zeros((), wf.dtype))
    return blocks.reshape(SHORTEN, heads, gph * per_group, gph * width)


def shorten_kernel(res_ref, rim_ref, wd_ref, q_ref, kv_ref):
    f32, bf16 = jnp.float32, jnp.bfloat16
    rows = res_ref.shape[0]
    tokens = rows // SHORTEN
    heads = q_ref.shape[0]
    hd = q_ref.shape[2]
    groups, span, outs = wd_ref.shape
    gph = groups // heads
    width = span // SHORTEN
    per_group = outs // 3
    j_i = lax.broadcasted_iota(jnp.int32, (tokens, rows), 0)
    r_i = lax.broadcasted_iota(jnp.int32, (tokens, rows), 1)
    first = lax.broadcasted_iota(jnp.int32, (tokens, 1), 0) == 0
    res = res_ref[...]
    picked = []
    for t in range(SHORTEN):
        sel = (r_i == SHORTEN * j_i + t - (SHORTEN - 1)).astype(bf16)
        x = jnp.dot(sel, res, preferred_element_type=f32).astype(bf16)
        if t < SHORTEN - 1:
            x = jnp.where(first, rim_ref[pl.ds(t, 1), :], x)
        picked.append(x)
    i_i = lax.broadcasted_iota(jnp.int32, (outs, 3 * hd), 0)
    n_i = lax.broadcasted_iota(jnp.int32, (outs, 3 * hd), 1)
    place = [
        (n_i == (i_i // per_group) * hd + g * per_group + i_i % per_group).astype(bf16)
        for g in range(gph)
    ]
    pair = 128 // width
    for k in range(heads):
        acc = None
        for m in range(gph // pair):
            for t in range(SHORTEN):
                pieces = []
                for e in range(pair):
                    g = m * pair + e
                    w = wd_ref[k * gph + g, pl.ds(t * width, width), :]
                    pieces.append(jnp.dot(w, place[g], preferred_element_type=f32).astype(bf16))
                wp = jnp.concatenate(pieces, axis=0)
                col = (k * gph + m * pair) * width
                part = jnp.dot(picked[t][:, col : col + 128], wp, preferred_element_type=f32)
                acc = part if acc is None else acc + part
        q_ref[k] = normalize(acc[:, :hd]).astype(bf16)
        kv_ref[0, 0, k] = normalize(acc[:, hd : 2 * hd]).astype(bf16)
        kv_ref[1, 0, k] = acc[:, 2 * hd :].astype(bf16)


def post_kernel(idx_ref, sharp_ref, q_ref, kv_ref, wup_ref, res_ref, oct_ref, out_ref, att_scr):
    me = idx_ref[0]
    heads, tq, hd = q_ref.shape
    f32, bf16 = jnp.float32, jnp.bfloat16
    nb = kv_ref.shape[1]
    qpos = me * tq + lax.broadcasted_iota(jnp.int32, (tq, nb * tq), 0)
    kpos = lax.broadcasted_iota(jnp.int32, (tq, nb * tq), 1)
    visible = kpos <= qpos
    for h in range(heads):
        q = q_ref[h]
        sharp = sharp_ref[h]
        keys = jnp.concatenate([kv_ref[0, d, h] for d in range(nb)], axis=0)
        vals = jnp.concatenate([kv_ref[1, d, h] for d in range(nb)], axis=0)
        s = lax.dot_general(q, keys, (((1,), (1,)), ((), ())), preferred_element_type=f32) * sharp
        w = jnp.where(visible, jnp.exp(s - sharp), jnp.zeros((), f32))
        den = jnp.sum(w, axis=1, keepdims=True)
        num = jnp.dot(w.astype(bf16), vals, preferred_element_type=f32)
        att_scr[:, h * hd : (h + 1) * hd] = (num / den).astype(bf16)

    rows, width = res_ref.shape
    row_blocks = rows // 128
    tok_blk = 128 // SHORTEN
    n_chunks = wup_ref.shape[1]
    cin = wup_ref.shape[2]
    cout = wup_ref.shape[3]
    r_i = lax.broadcasted_iota(jnp.int32, (128, tok_blk), 0)
    j_i = lax.broadcasted_iota(jnp.int32, (128, tok_blk), 1)
    for rb in range(row_blocks):
        a_blk = att_scr[pl.ds(rb * tok_blk, tok_blk), :]
        expanded = []
        for t in range(SHORTEN):
            sel = (r_i == SHORTEN * j_i + t).astype(bf16)
            expanded.append(jnp.dot(sel, a_blk, preferred_element_type=f32).astype(bf16))
        hid = []
        ss = jnp.zeros((128, 1), f32)
        for k in range(n_chunks):
            u = jnp.dot(expanded[0][:, k * cin : (k + 1) * cin], wup_ref[0, k], preferred_element_type=f32)
            for t in range(1, SHORTEN):
                u = u + jnp.dot(
                    expanded[t][:, k * cin : (k + 1) * cin], wup_ref[t, k], preferred_element_type=f32
                )
            hcol = res_ref[pl.ds(rb * 128, 128), pl.ds(k * cout, cout)].astype(f32) + u
            hid.append(hcol)
            ss = ss + jnp.sum(hcol * hcol, axis=1, keepdims=True)
        scale = lax.rsqrt(ss / width + 1e-05)
        acc = None
        for k in range(n_chunks):
            part = lax.dot_general(
                (hid[k] * scale).astype(bf16),
                oct_ref[:, pl.ds(k * cout, cout)],
                (((1,), (1,)), ((), ())),
                preferred_element_type=f32,
            )
            acc = part if acc is None else acc + part
        out_ref[pl.ds(rb * 128, 128), :] = (acc * width ** (-0.5)).astype(out_ref.dtype)


def on_device(
    residual_stream, octet_readout, downsampling_filter, sharpness_factor, widening_filter
):
    byte_rows = residual_stream.shape[0]
    groups = downsampling_filter.shape[0]
    per_group = downsampling_filter.shape[2] // 3
    attention_number = sharpness_factor.shape[0]
    head_size = groups * per_group // attention_number
    tokens_here = byte_rows // SHORTEN
    rim_rows = SHORTEN - 1
    left_rim = shifted_2(residual_stream[byte_rows - rim_rows :], "seq", 1)
    vmem = pl.BlockSpec(memory_space=pltpu.VMEM)
    smem = pl.BlockSpec(memory_space=pltpu.SMEM)
    queries, stacked = pl.pallas_call(
        shorten_kernel,
        out_shape=(
            jax.ShapeDtypeStruct((attention_number, tokens_here, head_size), jnp.bfloat16),
            jax.ShapeDtypeStruct((2, 1, attention_number, tokens_here, head_size), jnp.bfloat16),
        ),
        in_specs=[vmem, vmem, vmem],
        out_specs=(vmem, vmem),
        compiler_params=pltpu.CompilerParams(vmem_limit_bytes=60 * 1024 * 1024),
    )(residual_stream, left_rim, downsampling_filter)
    gathered = lax.all_gather(stacked, "seq", axis=1, tiled=True)
    my_index = lax.axis_index("seq").astype(jnp.int32).reshape(1)
    wup = widening_blocks(widening_filter, attention_number)
    return pl.pallas_call(
        post_kernel,
        out_shape=jax.ShapeDtypeStruct((byte_rows, octet_readout.shape[0]), jnp.bfloat16),
        in_specs=[smem, smem, vmem, vmem, vmem, vmem, vmem],
        out_specs=vmem,
        scratch_shapes=[pltpu.VMEM((tokens_here, attention_number * head_size), jnp.bfloat16)],
        compiler_params=pltpu.CompilerParams(vmem_limit_bytes=60 * 1024 * 1024),
    )(my_index, sharpness_factor, queries, gathered, wup, residual_stream, octet_readout)


def solution(mesh):
    in_specs = (P(("dp", "seq"), None), P(), P(), P(), P())
    out_specs = P(("dp", "seq"), None)
    return jax.shard_map(
        on_device, mesh=mesh, in_specs=in_specs, out_specs=out_specs, check_vma=False
    )
```

```python
import functools

import jax
import jax.numpy as jnp
from jax import lax
from jax.experimental import pallas as pl
from jax.experimental.pallas import tpu as pltpu
from jax.sharding import PartitionSpec as P

SHORTEN = 4


def shifted_2(array, axis, by):
    count = lax.axis_size(axis)
    pairs = [(i, i + by) for i in range(count) if 0 <= i + by < count]
    return lax.ppermute(array, axis, pairs)


def normalize(vectors):
    return vectors * lax.rsqrt(jnp.sum(vectors * vectors, axis=-1, keepdims=True) + 1e-06)


def widening_blocks(widening_filter, heads):
    groups, per_group, span = widening_filter.shape
    gph = groups // heads
    width = span // SHORTEN
    wf = widening_filter.reshape(heads, gph, per_group, SHORTEN, width)
    wf = wf.transpose(3, 0, 1, 2, 4)[:, :, :, :, None, :]
    eye = jnp.eye(gph, dtype=jnp.bool_)[:, None, :, None]
    blocks = jnp.where(eye, wf, jnp.zeros((), wf.dtype))
    return blocks.reshape(SHORTEN, heads, gph * per_group, gph * width)


def shorten_kernel(res_ref, rim_ref, wd_ref, q_ref, kv_ref, *, head0):
    f32, bf16 = jnp.float32, jnp.bfloat16
    rows = res_ref.shape[0]
    tokens = rows // SHORTEN
    heads = q_ref.shape[0]
    hd = q_ref.shape[2]
    groups, span, outs = wd_ref.shape
    width = span // SHORTEN
    per_group = outs // 3
    gph = hd // per_group
    j_i = lax.broadcasted_iota(jnp.int32, (tokens, rows), 0)
    r_i = lax.broadcasted_iota(jnp.int32, (tokens, rows), 1)
    first = lax.broadcasted_iota(jnp.int32, (tokens, 1), 0) == 0
    res = res_ref[...]
    picked = []
    for t in range(SHORTEN):
        sel = (r_i == SHORTEN * j_i + t - (SHORTEN - 1)).astype(bf16)
        x = jnp.dot(sel, res, preferred_element_type=f32).astype(bf16)
        if t < SHORTEN - 1:
            x = jnp.where(first, rim_ref[pl.ds(t, 1), :], x)
        picked.append(x)
    i_i = lax.broadcasted_iota(jnp.int32, (outs, 3 * hd), 0)
    n_i = lax.broadcasted_iota(jnp.int32, (outs, 3 * hd), 1)
    place = [
        (n_i == (i_i // per_group) * hd + g * per_group + i_i % per_group).astype(bf16)
        for g in range(gph)
    ]
    pair = 128 // width
    for kk in range(heads):
        k = head0 + kk
        acc = None
        for m in range(gph // pair):
            for t in range(SHORTEN):
                pieces = []
                for e in range(pair):
                    g = m * pair + e
                    w = wd_ref[k * gph + g, pl.ds(t * width, width), :]
                    pieces.append(jnp.dot(w, place[g], preferred_element_type=f32).astype(bf16))
                wp = jnp.concatenate(pieces, axis=0)
                col = (k * gph + m * pair) * width
                part = jnp.dot(picked[t][:, col : col + 128], wp, preferred_element_type=f32)
                acc = part if acc is None else acc + part
        q_ref[kk] = normalize(acc[:, :hd]).astype(bf16)
        kv_ref[0, 0, kk] = normalize(acc[:, hd : 2 * hd]).astype(bf16)
        kv_ref[1, 0, kk] = acc[:, 2 * hd :].astype(bf16)


def attend_heads(me, sharp_ref, head0, q_ref, kv_ref, att_ref, col0):
    f32, bf16 = jnp.float32, jnp.bfloat16
    heads, tq, hd = q_ref.shape
    nb = kv_ref.shape[1]
    qpos = me * tq + lax.broadcasted_iota(jnp.int32, (tq, nb * tq), 0)
    kpos = lax.broadcasted_iota(jnp.int32, (tq, nb * tq), 1)
    visible = kpos <= qpos
    for h in range(heads):
        q = q_ref[h]
        sharp = sharp_ref[head0 + h]
        keys = jnp.concatenate([kv_ref[0, d, h] for d in range(nb)], axis=0)
        vals = jnp.concatenate([kv_ref[1, d, h] for d in range(nb)], axis=0)
        s = lax.dot_general(q, keys, (((1,), (1,)), ((), ())), preferred_element_type=f32) * sharp
        w = jnp.where(visible, jnp.exp(s - sharp), jnp.zeros((), f32))
        den = jnp.sum(w, axis=1, keepdims=True)
        num = jnp.dot(w.astype(bf16), vals, preferred_element_type=f32)
        att_ref[:, col0 + h * hd : col0 + (h + 1) * hd] = (num / den).astype(bf16)


def first_kernel(idx_ref, sharp_ref, q_ref, kv_ref, att_ref):
    attend_heads(idx_ref[0], sharp_ref, 0, q_ref, kv_ref, att_ref, 0)


def post_kernel(idx_ref, sharp_ref, q_ref, kv_ref, early_ref, wup_ref, res_ref, oct_ref, out_ref, att_scr):
    f32, bf16 = jnp.float32, jnp.bfloat16
    done = early_ref.shape[1]
    heads_done = sharp_ref.shape[0] - q_ref.shape[0]
    att_scr[:, :done] = early_ref[...]
    attend_heads(idx_ref[0], sharp_ref, heads_done, q_ref, kv_ref, att_scr, done)

    rows, width = res_ref.shape
    row_blocks = rows // 128
    tok_blk = 128 // SHORTEN
    n_chunks = wup_ref.shape[1]
    cin = wup_ref.shape[2]
    cout = wup_ref.shape[3]
    r_i = lax.broadcasted_iota(jnp.int32, (128, tok_blk), 0)
    j_i = lax.broadcasted_iota(jnp.int32, (128, tok_blk), 1)
    for rb in range(row_blocks):
        a_blk = att_scr[pl.ds(rb * tok_blk, tok_blk), :]
        expanded = []
        for t in range(SHORTEN):
            sel = (r_i == SHORTEN * j_i + t).astype(bf16)
            expanded.append(jnp.dot(sel, a_blk, preferred_element_type=f32).astype(bf16))
        hid = []
        ss = jnp.zeros((128, 1), f32)
        for k in range(n_chunks):
            u = jnp.dot(expanded[0][:, k * cin : (k + 1) * cin], wup_ref[0, k], preferred_element_type=f32)
            for t in range(1, SHORTEN):
                u = u + jnp.dot(
                    expanded[t][:, k * cin : (k + 1) * cin], wup_ref[t, k], preferred_element_type=f32
                )
            hcol = res_ref[pl.ds(rb * 128, 128), pl.ds(k * cout, cout)].astype(f32) + u
            hid.append(hcol)
            ss = ss + jnp.sum(hcol * hcol, axis=1, keepdims=True)
        scale = lax.rsqrt(ss / width + 1e-05)
        acc = None
        for k in range(n_chunks):
            part = lax.dot_general(
                (hid[k] * scale).astype(bf16),
                oct_ref[:, pl.ds(k * cout, cout)],
                (((1,), (1,)), ((), ())),
                preferred_element_type=f32,
            )
            acc = part if acc is None else acc + part
        out_ref[pl.ds(rb * 128, 128), :] = (acc * width ** (-0.5)).astype(out_ref.dtype)


def on_device(
    residual_stream, octet_readout, downsampling_filter, sharpness_factor, widening_filter
):
    byte_rows = residual_stream.shape[0]
    groups = downsampling_filter.shape[0]
    per_group = downsampling_filter.shape[2] // 3
    attention_number = sharpness_factor.shape[0]
    head_size = groups * per_group // attention_number
    tokens_here = byte_rows // SHORTEN
    rim_rows = SHORTEN - 1
    left_rim = shifted_2(residual_stream[byte_rows - rim_rows :], "seq", 1)
    vmem = pl.BlockSpec(memory_space=pltpu.VMEM)
    smem = pl.BlockSpec(memory_space=pltpu.SMEM)
    params = pltpu.CompilerParams(vmem_limit_bytes=60 * 1024 * 1024)
    half = attention_number // 2
    my_index = lax.axis_index("seq").astype(jnp.int32).reshape(1)

    def shorten_half(head0):
        return pl.pallas_call(
            functools.partial(shorten_kernel, head0=head0),
            out_shape=(
                jax.ShapeDtypeStruct((half, tokens_here, head_size), jnp.bfloat16),
                jax.ShapeDtypeStruct((2, 1, half, tokens_here, head_size), jnp.bfloat16),
            ),
            in_specs=[vmem, vmem, vmem],
            out_specs=(vmem, vmem),
            compiler_params=params,
        )(residual_stream, left_rim, downsampling_filter)

    q_a, kv_a = shorten_half(0)
    gathered_a = lax.all_gather(kv_a, "seq", axis=1, tiled=True)
    q_b, kv_b = shorten_half(half)
    gathered_b = lax.all_gather(kv_b, "seq", axis=1, tiled=True)
    early = pl.pallas_call(
        first_kernel,
        out_shape=jax.ShapeDtypeStruct((tokens_here, half * head_size), jnp.bfloat16),
        in_specs=[smem, smem, vmem, vmem],
        out_specs=vmem,
        compiler_params=params,
    )(my_index, sharpness_factor, q_a, gathered_a)
    wup = widening_blocks(widening_filter, attention_number)
    return pl.pallas_call(
        post_kernel,
        out_shape=jax.ShapeDtypeStruct((byte_rows, octet_readout.shape[0]), jnp.bfloat16),
        in_specs=[smem, smem, vmem, vmem, vmem, vmem, vmem, vmem],
        out_specs=vmem,
        scratch_shapes=[pltpu.VMEM((tokens_here, attention_number * head_size), jnp.bfloat16)],
        compiler_params=params,
    )(my_index, sharpness_factor, q_b, gathered_b, early, wup, residual_stream, octet_readout)


def solution(mesh):
    in_specs = (P(("dp", "seq"), None), P(), P(), P(), P())
    out_specs = P(("dp", "seq"), None)
    return jax.shard_map(
        on_device, mesh=mesh, in_specs=in_specs, out_specs=out_specs, check_vma=False
    )
```

```python
import functools

import jax
import jax.numpy as jnp
from jax import lax
from jax.experimental import pallas as pl
from jax.experimental.pallas import tpu as pltpu
from jax.sharding import PartitionSpec as P

SHORTEN = 4


def shifted_2(array, axis, by):
    count = lax.axis_size(axis)
    pairs = [(i, i + by) for i in range(count) if 0 <= i + by < count]
    return lax.ppermute(array, axis, pairs)


def normalize(vectors):
    return vectors * lax.rsqrt(jnp.sum(vectors * vectors, axis=-1, keepdims=True) + 1e-06)


def widening_blocks(widening_filter, heads):
    groups, per_group, span = widening_filter.shape
    gph = groups // heads
    width = span // SHORTEN
    wf = widening_filter.reshape(heads, gph, per_group, SHORTEN, width)
    wf = wf.transpose(3, 0, 1, 2, 4)[:, :, :, :, None, :]
    eye = jnp.eye(gph, dtype=jnp.bool_)[:, None, :, None]
    blocks = jnp.where(eye, wf, jnp.zeros((), wf.dtype))
    return blocks.reshape(SHORTEN, heads, gph * per_group, gph * width)


def shorten_kernel(res_ref, rim_ref, wd_ref, *outs, parts):
    f32, bf16 = jnp.float32, jnp.bfloat16
    rows = res_ref.shape[0]
    tokens = rows // SHORTEN
    heads = outs[0].shape[-3]
    hd = outs[0].shape[-1]
    groups, span, channels = wd_ref.shape
    gph = groups // heads
    width = span // SHORTEN
    per_group = channels // 3
    j_i = lax.broadcasted_iota(jnp.int32, (tokens, rows), 0)
    r_i = lax.broadcasted_iota(jnp.int32, (tokens, rows), 1)
    first = lax.broadcasted_iota(jnp.int32, (tokens, 1), 0) == 0
    res = res_ref[...]
    picked = []
    for t in range(SHORTEN):
        sel = (r_i == SHORTEN * j_i + t - (SHORTEN - 1)).astype(bf16)
        x = jnp.dot(sel, res, preferred_element_type=f32).astype(bf16)
        if t < SHORTEN - 1:
            x = jnp.where(first, rim_ref[pl.ds(t, 1), :], x)
        picked.append(x)
    first_part = 0 if parts == "q" else 1
    n_parts = 1 if parts == "q" else 2
    i_i = lax.broadcasted_iota(jnp.int32, (n_parts * per_group, n_parts * hd), 0)
    n_i = lax.broadcasted_iota(jnp.int32, (n_parts * per_group, n_parts * hd), 1)
    place = [
        (n_i == (i_i // per_group) * hd + g * per_group + i_i % per_group).astype(bf16)
        for g in range(gph)
    ]
    pair = 128 // width
    for k in range(heads):
        acc = None
        for m in range(gph // pair):
            for t in range(SHORTEN):
                pieces = []
                for e in range(pair):
                    g = m * pair + e
                    w = wd_ref[k * gph + g, pl.ds(t * width, width), pl.ds(first_part * per_group, n_parts * per_group)]
                    pieces.append(jnp.dot(w, place[g], preferred_element_type=f32).astype(bf16))
                wp = jnp.concatenate(pieces, axis=0)
                col = (k * gph + m * pair) * width
                part = jnp.dot(picked[t][:, col : col + 128], wp, preferred_element_type=f32)
                acc = part if acc is None else acc + part
        if parts == "q":
            outs[0][k] = normalize(acc[:, :hd]).astype(bf16)
        else:
            outs[0][0, 0, k] = normalize(acc[:, :hd]).astype(bf16)
            outs[0][1, 0, k] = acc[:, hd:].astype(bf16)


def post_kernel(idx_ref, sharp_ref, q_ref, kv_ref, wup_ref, res_ref, oct_ref, out_ref, att_scr):
    me = idx_ref[0]
    heads, tq, hd = q_ref.shape
    f32, bf16 = jnp.float32, jnp.bfloat16
    nb = kv_ref.shape[1]
    qpos = me * tq + lax.broadcasted_iota(jnp.int32, (tq, nb * tq), 0)
    kpos = lax.broadcasted_iota(jnp.int32, (tq, nb * tq), 1)
    visible = kpos <= qpos
    for h in range(heads):
        q = q_ref[h]
        sharp = sharp_ref[h]
        keys = jnp.concatenate([kv_ref[0, d, h] for d in range(nb)], axis=0)
        vals = jnp.concatenate([kv_ref[1, d, h] for d in range(nb)], axis=0)
        s = lax.dot_general(q, keys, (((1,), (1,)), ((), ())), preferred_element_type=f32) * sharp
        w = jnp.where(visible, jnp.exp(s - sharp), jnp.zeros((), f32))
        den = jnp.sum(w, axis=1, keepdims=True)
        num = jnp.dot(w.astype(bf16), vals, preferred_element_type=f32)
        att_scr[:, h * hd : (h + 1) * hd] = (num / den).astype(bf16)

    rows, width = res_ref.shape
    row_blocks = rows // 128
    tok_blk = 128 // SHORTEN
    n_chunks = wup_ref.shape[1]
    cin = wup_ref.shape[2]
    cout = wup_ref.shape[3]
    r_i = lax.broadcasted_iota(jnp.int32, (128, tok_blk), 0)
    j_i = lax.broadcasted_iota(jnp.int32, (128, tok_blk), 1)
    for rb in range(row_blocks):
        a_blk = att_scr[pl.ds(rb * tok_blk, tok_blk), :]
        expanded = []
        for t in range(SHORTEN):
            sel = (r_i == SHORTEN * j_i + t).astype(bf16)
            expanded.append(jnp.dot(sel, a_blk, preferred_element_type=f32).astype(bf16))
        hid = []
        ss = jnp.zeros((128, 1), f32)
        for k in range(n_chunks):
            u = jnp.dot(expanded[0][:, k * cin : (k + 1) * cin], wup_ref[0, k], preferred_element_type=f32)
            for t in range(1, SHORTEN):
                u = u + jnp.dot(
                    expanded[t][:, k * cin : (k + 1) * cin], wup_ref[t, k], preferred_element_type=f32
                )
            hcol = res_ref[pl.ds(rb * 128, 128), pl.ds(k * cout, cout)].astype(f32) + u
            hid.append(hcol)
            ss = ss + jnp.sum(hcol * hcol, axis=1, keepdims=True)
        scale = lax.rsqrt(ss / width + 1e-05)
        acc = None
        for k in range(n_chunks):
            part = lax.dot_general(
                (hid[k] * scale).astype(bf16),
                oct_ref[:, pl.ds(k * cout, cout)],
                (((1,), (1,)), ((), ())),
                preferred_element_type=f32,
            )
            acc = part if acc is None else acc + part
        out_ref[pl.ds(rb * 128, 128), :] = (acc * width ** (-0.5)).astype(out_ref.dtype)


def on_device(
    residual_stream, octet_readout, downsampling_filter, sharpness_factor, widening_filter
):
    byte_rows = residual_stream.shape[0]
    groups = downsampling_filter.shape[0]
    per_group = downsampling_filter.shape[2] // 3
    attention_number = sharpness_factor.shape[0]
    head_size = groups * per_group // attention_number
    tokens_here = byte_rows // SHORTEN
    rim_rows = SHORTEN - 1
    left_rim = shifted_2(residual_stream[byte_rows - rim_rows :], "seq", 1)
    vmem = pl.BlockSpec(memory_space=pltpu.VMEM)
    smem = pl.BlockSpec(memory_space=pltpu.SMEM)
    params = pltpu.CompilerParams(vmem_limit_bytes=60 * 1024 * 1024)
    stacked = pl.pallas_call(
        functools.partial(shorten_kernel, parts="kv"),
        out_shape=jax.ShapeDtypeStruct((2, 1, attention_number, tokens_here, head_size), jnp.bfloat16),
        in_specs=[vmem, vmem, vmem],
        out_specs=vmem,
        compiler_params=params,
    )(residual_stream, left_rim, downsampling_filter)
    gathered = lax.all_gather(stacked, "seq", axis=1, tiled=True)
    queries = pl.pallas_call(
        functools.partial(shorten_kernel, parts="q"),
        out_shape=jax.ShapeDtypeStruct((attention_number, tokens_here, head_size), jnp.bfloat16),
        in_specs=[vmem, vmem, vmem],
        out_specs=vmem,
        compiler_params=params,
    )(residual_stream, left_rim, downsampling_filter)
    my_index = lax.axis_index("seq").astype(jnp.int32).reshape(1)
    wup = widening_blocks(widening_filter, attention_number)
    return pl.pallas_call(
        post_kernel,
        out_shape=jax.ShapeDtypeStruct((byte_rows, octet_readout.shape[0]), jnp.bfloat16),
        in_specs=[smem, smem, vmem, vmem, vmem, vmem, vmem],
        out_specs=vmem,
        scratch_shapes=[pltpu.VMEM((tokens_here, attention_number * head_size), jnp.bfloat16)],
        compiler_params=pltpu.CompilerParams(vmem_limit_bytes=60 * 1024 * 1024),
    )(my_index, sharpness_factor, queries, gathered, wup, residual_stream, octet_readout)


def solution(mesh):
    in_specs = (P(("dp", "seq"), None), P(), P(), P(), P())
    out_specs = P(("dp", "seq"), None)
    return jax.shard_map(
        on_device, mesh=mesh, in_specs=in_specs, out_specs=out_specs, check_vma=False
    )
```

```python
import functools

import jax
import jax.numpy as jnp
from jax import lax
from jax.experimental import pallas as pl
from jax.experimental.pallas import tpu as pltpu
from jax.sharding import PartitionSpec as P

SHORTEN = 4


def shifted_2(array, axis, by):
    count = lax.axis_size(axis)
    pairs = [(i, i + by) for i in range(count) if 0 <= i + by < count]
    return lax.ppermute(array, axis, pairs)


def normalize(vectors):
    return vectors * lax.rsqrt(jnp.sum(vectors * vectors, axis=-1, keepdims=True) + 1e-06)


def widening_blocks(widening_filter, heads):
    groups, per_group, span = widening_filter.shape
    gph = groups // heads
    width = span // SHORTEN
    wf = widening_filter.reshape(heads, gph, per_group, SHORTEN, width)
    wf = wf.transpose(3, 0, 1, 2, 4)[:, :, :, :, None, :]
    eye = jnp.eye(gph, dtype=jnp.bool_)[:, None, :, None]
    blocks = jnp.where(eye, wf, jnp.zeros((), wf.dtype))
    return blocks.reshape(SHORTEN, heads, gph * per_group, gph * width)


def shorten_kernel(res_ref, rim_ref, wd_ref, *outs, parts):
    f32, bf16 = jnp.float32, jnp.bfloat16
    rows = res_ref.shape[0]
    tokens = rows // SHORTEN
    heads = outs[0].shape[-3]
    hd = outs[0].shape[-1]
    groups, span, channels = wd_ref.shape
    gph = groups // heads
    width = span // SHORTEN
    per_group = channels // 3
    j_i = lax.broadcasted_iota(jnp.int32, (tokens, rows), 0)
    r_i = lax.broadcasted_iota(jnp.int32, (tokens, rows), 1)
    first = lax.broadcasted_iota(jnp.int32, (tokens, 1), 0) == 0
    res = res_ref[...]
    picked = []
    for t in range(SHORTEN):
        sel = (r_i == SHORTEN * j_i + t - (SHORTEN - 1)).astype(bf16)
        x = jnp.dot(sel, res, preferred_element_type=f32).astype(bf16)
        if t < SHORTEN - 1:
            x = jnp.where(first, rim_ref[pl.ds(t, 1), :], x)
        picked.append(x)
    first_part = 0 if parts == "q" else 1
    n_parts = 1 if parts == "q" else 2
    i_i = lax.broadcasted_iota(jnp.int32, (n_parts * per_group, n_parts * hd), 0)
    n_i = lax.broadcasted_iota(jnp.int32, (n_parts * per_group, n_parts * hd), 1)
    place = [
        (n_i == (i_i // per_group) * hd + g * per_group + i_i % per_group).astype(bf16)
        for g in range(gph)
    ]
    pair = 128 // width
    for k in range(heads):
        acc = None
        for m in range(gph // pair):
            for t in range(SHORTEN):
                pieces = []
                for e in range(pair):
                    g = m * pair + e
                    w = wd_ref[k * gph + g, pl.ds(t * width, width), pl.ds(first_part * per_group, n_parts * per_group)]
                    pieces.append(jnp.dot(w, place[g], preferred_element_type=f32).astype(bf16))
                wp = jnp.concatenate(pieces, axis=0)
                col = (k * gph + m * pair) * width
                part = jnp.dot(picked[t][:, col : col + 128], wp, preferred_element_type=f32)
                acc = part if acc is None else acc + part
        if parts == "q":
            outs[0][k] = normalize(acc[:, :hd]).astype(bf16)
        else:
            outs[0][0, 0, k] = normalize(acc[:, :hd]).T.astype(bf16)
            outs[0][1, 0, k] = acc[:, hd:].astype(bf16)


def post_kernel(idx_ref, sharp_ref, q_ref, kv_ref, wup_ref, res_ref, oct_ref, out_ref, att_scr):
    me = idx_ref[0]
    heads, tq, hd = q_ref.shape
    f32, bf16 = jnp.float32, jnp.bfloat16
    nb = kv_ref.shape[1]
    qpos = me * tq + lax.broadcasted_iota(jnp.int32, (tq, nb * tq), 0)
    kpos = lax.broadcasted_iota(jnp.int32, (tq, nb * tq), 1)
    visible = kpos <= qpos
    for h in range(heads):
        q = q_ref[h]
        sharp = sharp_ref[h]
        keys_t = jnp.concatenate([kv_ref[0, d, h] for d in range(nb)], axis=1)
        vals = jnp.concatenate([kv_ref[1, d, h] for d in range(nb)], axis=0)
        s = jnp.dot(q, keys_t, preferred_element_type=f32) * sharp
        w = jnp.where(visible, jnp.exp(s - sharp), jnp.zeros((), f32))
        den = jnp.sum(w, axis=1, keepdims=True)
        num = jnp.dot(w.astype(bf16), vals, preferred_element_type=f32)
        att_scr[:, h * hd : (h + 1) * hd] = (num / den).astype(bf16)

    rows, width = res_ref.shape
    row_blocks = rows // 128
    tok_blk = 128 // SHORTEN
    n_chunks = wup_ref.shape[1]
    cin = wup_ref.shape[2]
    cout = wup_ref.shape[3]
    r_i = lax.broadcasted_iota(jnp.int32, (128, tok_blk), 0)
    j_i = lax.broadcasted_iota(jnp.int32, (128, tok_blk), 1)
    for rb in range(row_blocks):
        a_blk = att_scr[pl.ds(rb * tok_blk, tok_blk), :]
        expanded = []
        for t in range(SHORTEN):
            sel = (r_i == SHORTEN * j_i + t).astype(bf16)
            expanded.append(jnp.dot(sel, a_blk, preferred_element_type=f32).astype(bf16))
        hid = []
        ss = jnp.zeros((128, 1), f32)
        for k in range(n_chunks):
            u = jnp.dot(expanded[0][:, k * cin : (k + 1) * cin], wup_ref[0, k], preferred_element_type=f32)
            for t in range(1, SHORTEN):
                u = u + jnp.dot(
                    expanded[t][:, k * cin : (k + 1) * cin], wup_ref[t, k], preferred_element_type=f32
                )
            hcol = res_ref[pl.ds(rb * 128, 128), pl.ds(k * cout, cout)].astype(f32) + u
            hid.append(hcol)
            ss = ss + jnp.sum(hcol * hcol, axis=1, keepdims=True)
        scale = lax.rsqrt(ss / width + 1e-05)
        acc = None
        for k in range(n_chunks):
            part = jnp.dot(
                (hid[k] * scale).astype(bf16),
                oct_ref[pl.ds(k * cout, cout), :],
                preferred_element_type=f32,
            )
            acc = part if acc is None else acc + part
        out_ref[pl.ds(rb * 128, 128), :] = (acc * width ** (-0.5)).astype(out_ref.dtype)


def on_device(
    residual_stream, octet_readout, downsampling_filter, sharpness_factor, widening_filter
):
    byte_rows = residual_stream.shape[0]
    groups = downsampling_filter.shape[0]
    per_group = downsampling_filter.shape[2] // 3
    attention_number = sharpness_factor.shape[0]
    head_size = groups * per_group // attention_number
    tokens_here = byte_rows // SHORTEN
    rim_rows = SHORTEN - 1
    left_rim = shifted_2(residual_stream[byte_rows - rim_rows :], "seq", 1)
    vmem = pl.BlockSpec(memory_space=pltpu.VMEM)
    smem = pl.BlockSpec(memory_space=pltpu.SMEM)
    params = pltpu.CompilerParams(vmem_limit_bytes=60 * 1024 * 1024)
    stacked = pl.pallas_call(
        functools.partial(shorten_kernel, parts="kv"),
        out_shape=jax.ShapeDtypeStruct((2, 1, attention_number, tokens_here, head_size), jnp.bfloat16),
        in_specs=[vmem, vmem, vmem],
        out_specs=vmem,
        compiler_params=params,
    )(residual_stream, left_rim, downsampling_filter)
    gathered = lax.all_gather(stacked, "seq", axis=1, tiled=True)
    queries = pl.pallas_call(
        functools.partial(shorten_kernel, parts="q"),
        out_shape=jax.ShapeDtypeStruct((attention_number, tokens_here, head_size), jnp.bfloat16),
        in_specs=[vmem, vmem, vmem],
        out_specs=vmem,
        compiler_params=params,
    )(residual_stream, left_rim, downsampling_filter)
    my_index = lax.axis_index("seq").astype(jnp.int32).reshape(1)
    wup = widening_blocks(widening_filter, attention_number)
    return pl.pallas_call(
        post_kernel,
        out_shape=jax.ShapeDtypeStruct((byte_rows, octet_readout.shape[0]), jnp.bfloat16),
        in_specs=[smem, smem, vmem, vmem, vmem, vmem, vmem],
        out_specs=vmem,
        scratch_shapes=[pltpu.VMEM((tokens_here, attention_number * head_size), jnp.bfloat16)],
        compiler_params=pltpu.CompilerParams(vmem_limit_bytes=60 * 1024 * 1024),
    )(my_index, sharpness_factor, queries, gathered, wup, residual_stream, octet_readout.T)


def solution(mesh):
    in_specs = (P(("dp", "seq"), None), P(), P(), P(), P())
    out_specs = P(("dp", "seq"), None)
    return jax.shard_map(
        on_device, mesh=mesh, in_specs=in_specs, out_specs=out_specs, check_vma=False
    )
```

```python
import functools

import jax
import jax.numpy as jnp
from jax import lax
from jax.experimental import pallas as pl
from jax.experimental.pallas import tpu as pltpu
from jax.sharding import PartitionSpec as P

SHORTEN = 4


def shifted_2(array, axis, by):
    count = lax.axis_size(axis)
    pairs = [(i, i + by) for i in range(count) if 0 <= i + by < count]
    return lax.ppermute(array, axis, pairs)


def normalize(vectors):
    return vectors * lax.rsqrt(jnp.sum(vectors * vectors, axis=-1, keepdims=True) + 1e-06)


def widening_blocks(widening_filter, heads):
    groups, per_group, span = widening_filter.shape
    gph = groups // heads
    width = span // SHORTEN
    wf = widening_filter.reshape(heads, gph, per_group, SHORTEN, width)
    wf = wf.transpose(3, 0, 1, 2, 4)[:, :, :, :, None, :]
    eye = jnp.eye(gph, dtype=jnp.bool_)[:, None, :, None]
    blocks = jnp.where(eye, wf, jnp.zeros((), wf.dtype))
    return blocks.reshape(SHORTEN, heads, gph * per_group, gph * width)


def shorten_kernel(res_ref, rim_ref, wd_ref, *outs, parts):
    f32, bf16 = jnp.float32, jnp.bfloat16
    rows = res_ref.shape[0]
    tokens = rows // SHORTEN
    heads = outs[0].shape[-3]
    hd = outs[0].shape[-1]
    groups, channels, span = wd_ref.shape
    gph = groups // heads
    width = span // SHORTEN
    per_group = channels // 3
    j_i = lax.broadcasted_iota(jnp.int32, (tokens, rows), 0)
    r_i = lax.broadcasted_iota(jnp.int32, (tokens, rows), 1)
    first = lax.broadcasted_iota(jnp.int32, (tokens, 1), 0) == 0
    res = res_ref[...]
    picked = []
    for t in range(SHORTEN):
        sel = (r_i == SHORTEN * j_i + t - (SHORTEN - 1)).astype(bf16)
        x = jnp.dot(sel, res, preferred_element_type=f32).astype(bf16)
        if t < SHORTEN - 1:
            x = jnp.where(first, rim_ref[pl.ds(t, 1), :], x)
        picked.append(x)
    first_part = 0 if parts == "q" else 1
    n_parts = 1 if parts == "q" else 2
    i_i = lax.broadcasted_iota(jnp.int32, (n_parts * per_group, n_parts * hd), 0)
    n_i = lax.broadcasted_iota(jnp.int32, (n_parts * per_group, n_parts * hd), 1)
    place = [
        (n_i == (i_i // per_group) * hd + g * per_group + i_i % per_group).astype(bf16)
        for g in range(gph)
    ]
    pair = 128 // width
    for k in range(heads):
        acc = None
        for m in range(gph // pair):
            for t in range(SHORTEN):
                pieces = []
                for e in range(pair):
                    g = m * pair + e
                    w = wd_ref[k * gph + g, pl.ds(first_part * per_group, n_parts * per_group), pl.ds(t * width, width)]
                    pieces.append(lax.dot_general(
                        w, place[g], (((0,), (0,)), ((), ())), preferred_element_type=f32
                    ).astype(bf16))
                wp = jnp.concatenate(pieces, axis=0)
                col = (k * gph + m * pair) * width
                part = jnp.dot(picked[t][:, col : col + 128], wp, preferred_element_type=f32)
                acc = part if acc is None else acc + part
        if parts == "q":
            outs[0][k] = normalize(acc[:, :hd]).astype(bf16)
        else:
            outs[0][0, 0, k] = normalize(acc[:, :hd]).T.astype(bf16)
            outs[0][1, 0, k] = acc[:, hd:].astype(bf16)


def post_kernel(idx_ref, sharp_ref, q_ref, kv_ref, wup_ref, res_ref, oct_ref, out_ref, att_scr):
    me = idx_ref[0]
    heads, tq, hd = q_ref.shape
    f32, bf16 = jnp.float32, jnp.bfloat16
    nb = kv_ref.shape[1]
    qpos = me * tq + lax.broadcasted_iota(jnp.int32, (tq, nb * tq), 0)
    kpos = lax.broadcasted_iota(jnp.int32, (tq, nb * tq), 1)
    visible = kpos <= qpos
    for h in range(heads):
        q = q_ref[h]
        sharp = sharp_ref[h]
        keys_t = jnp.concatenate([kv_ref[0, d, h] for d in range(nb)], axis=1)
        vals = jnp.concatenate([kv_ref[1, d, h] for d in range(nb)], axis=0)
        s = jnp.dot(q, keys_t, preferred_element_type=f32) * sharp
        w = jnp.where(visible, jnp.exp(s - sharp), jnp.zeros((), f32))
        den = jnp.sum(w, axis=1, keepdims=True)
        num = jnp.dot(w.astype(bf16), vals, preferred_element_type=f32)
        att_scr[:, h * hd : (h + 1) * hd] = (num / den).astype(bf16)

    rows, width = res_ref.shape
    row_blocks = rows // 128
    tok_blk = 128 // SHORTEN
    n_chunks = wup_ref.shape[1]
    cin = wup_ref.shape[2]
    cout = wup_ref.shape[3]
    r_i = lax.broadcasted_iota(jnp.int32, (128, tok_blk), 0)
    j_i = lax.broadcasted_iota(jnp.int32, (128, tok_blk), 1)
    for rb in range(row_blocks):
        a_blk = att_scr[pl.ds(rb * tok_blk, tok_blk), :]
        expanded = []
        for t in range(SHORTEN):
            sel = (r_i == SHORTEN * j_i + t).astype(bf16)
            expanded.append(jnp.dot(sel, a_blk, preferred_element_type=f32).astype(bf16))
        hid = []
        ss = jnp.zeros((128, 1), f32)
        for k in range(n_chunks):
            u = jnp.dot(expanded[0][:, k * cin : (k + 1) * cin], wup_ref[0, k], preferred_element_type=f32)
            for t in range(1, SHORTEN):
                u = u + jnp.dot(
                    expanded[t][:, k * cin : (k + 1) * cin], wup_ref[t, k], preferred_element_type=f32
                )
            hcol = res_ref[pl.ds(rb * 128, 128), pl.ds(k * cout, cout)].astype(f32) + u
            hid.append(hcol)
            ss = ss + jnp.sum(hcol * hcol, axis=1, keepdims=True)
        scale = lax.rsqrt(ss / width + 1e-05)
        acc = None
        for k in range(n_chunks):
            part = jnp.dot(
                (hid[k] * scale).astype(bf16),
                oct_ref[pl.ds(k * cout, cout), :],
                preferred_element_type=f32,
            )
            acc = part if acc is None else acc + part
        out_ref[pl.ds(rb * 128, 128), :] = (acc * width ** (-0.5)).astype(out_ref.dtype)


def on_device(
    residual_stream, octet_readout, downsampling_filter, sharpness_factor, widening_filter
):
    byte_rows = residual_stream.shape[0]
    groups = downsampling_filter.shape[0]
    per_group = downsampling_filter.shape[2] // 3
    attention_number = sharpness_factor.shape[0]
    head_size = groups * per_group // attention_number
    tokens_here = byte_rows // SHORTEN
    rim_rows = SHORTEN - 1
    left_rim = shifted_2(residual_stream[byte_rows - rim_rows :], "seq", 1)
    vmem = pl.BlockSpec(memory_space=pltpu.VMEM)
    smem = pl.BlockSpec(memory_space=pltpu.SMEM)
    params = pltpu.CompilerParams(vmem_limit_bytes=60 * 1024 * 1024)
    filter_t = jnp.swapaxes(downsampling_filter, 1, 2)
    stacked = pl.pallas_call(
        functools.partial(shorten_kernel, parts="kv"),
        out_shape=jax.ShapeDtypeStruct((2, 1, attention_number, tokens_here, head_size), jnp.bfloat16),
        in_specs=[vmem, vmem, vmem],
        out_specs=vmem,
        compiler_params=params,
    )(residual_stream, left_rim, filter_t)
    gathered = lax.all_gather(stacked, "seq", axis=1, tiled=True)
    queries = pl.pallas_call(
        functools.partial(shorten_kernel, parts="q"),
        out_shape=jax.ShapeDtypeStruct((attention_number, tokens_here, head_size), jnp.bfloat16),
        in_specs=[vmem, vmem, vmem],
        out_specs=vmem,
        compiler_params=params,
    )(residual_stream, left_rim, filter_t)
    my_index = lax.axis_index("seq").astype(jnp.int32).reshape(1)
    wup = widening_blocks(widening_filter, attention_number)
    return pl.pallas_call(
        post_kernel,
        out_shape=jax.ShapeDtypeStruct((byte_rows, octet_readout.shape[0]), jnp.bfloat16),
        in_specs=[smem, smem, vmem, vmem, vmem, vmem, vmem],
        out_specs=vmem,
        scratch_shapes=[pltpu.VMEM((tokens_here, attention_number * head_size), jnp.bfloat16)],
        compiler_params=pltpu.CompilerParams(vmem_limit_bytes=60 * 1024 * 1024),
    )(my_index, sharpness_factor, queries, gathered, wup, residual_stream, octet_readout.T)


def solution(mesh):
    in_specs = (P(("dp", "seq"), None), P(), P(), P(), P())
    out_specs = P(("dp", "seq"), None)
    return jax.shard_map(
        on_device, mesh=mesh, in_specs=in_specs, out_specs=out_specs, check_vma=False
    )
```

```python
import functools

import jax
import jax.numpy as jnp
from jax import lax
from jax.experimental import pallas as pl
from jax.experimental.pallas import tpu as pltpu
from jax.sharding import PartitionSpec as P

SHORTEN = 4


def shifted_2(array, axis, by):
    count = lax.axis_size(axis)
    pairs = [(i, i + by) for i in range(count) if 0 <= i + by < count]
    return lax.ppermute(array, axis, pairs)


def normalize(vectors):
    return vectors * lax.rsqrt(jnp.sum(vectors * vectors, axis=-1, keepdims=True) + 1e-06)


def widening_blocks(widening_filter, heads):
    groups, per_group, span = widening_filter.shape
    gph = groups // heads
    width = span // SHORTEN
    wf = widening_filter.reshape(heads, gph, per_group, SHORTEN, width)
    wf = wf.transpose(3, 0, 1, 2, 4)[:, :, :, :, None, :]
    eye = jnp.eye(gph, dtype=jnp.bool_)[:, None, :, None]
    blocks = jnp.where(eye, wf, jnp.zeros((), wf.dtype))
    blocks = blocks.reshape(SHORTEN, heads, gph * per_group, gph * width).transpose(1, 0, 2, 3)
    return blocks.reshape(heads, SHORTEN * gph * per_group, gph * width)


def shorten_kernel(res_ref, rim_ref, wd_ref, *outs, parts):
    f32, bf16 = jnp.float32, jnp.bfloat16
    rows = res_ref.shape[0]
    tokens = rows // SHORTEN
    heads = outs[0].shape[-3]
    hd = outs[0].shape[-1]
    groups, channels, span = wd_ref.shape
    gph = groups // heads
    width = span // SHORTEN
    per_group = channels // 3
    j_i = lax.broadcasted_iota(jnp.int32, (tokens, rows), 0)
    r_i = lax.broadcasted_iota(jnp.int32, (tokens, rows), 1)
    first = lax.broadcasted_iota(jnp.int32, (tokens, 1), 0) == 0
    res = res_ref[...]
    picked = []
    for t in range(SHORTEN):
        sel = (r_i == SHORTEN * j_i + t - (SHORTEN - 1)).astype(bf16)
        x = jnp.dot(sel, res, preferred_element_type=f32).astype(bf16)
        if t < SHORTEN - 1:
            x = jnp.where(first, rim_ref[pl.ds(t, 1), :], x)
        picked.append(x)
    first_part = 0 if parts == "q" else 1
    n_parts = 1 if parts == "q" else 2
    i_i = lax.broadcasted_iota(jnp.int32, (n_parts * per_group, n_parts * hd), 0)
    n_i = lax.broadcasted_iota(jnp.int32, (n_parts * per_group, n_parts * hd), 1)
    place = [
        (n_i == (i_i // per_group) * hd + g * per_group + i_i % per_group).astype(bf16)
        for g in range(gph)
    ]
    pair = 128 // width
    for k in range(heads):
        acc = None
        for m in range(gph // pair):
            for t in range(SHORTEN):
                pieces = []
                for e in range(pair):
                    g = m * pair + e
                    w = wd_ref[k * gph + g, pl.ds(first_part * per_group, n_parts * per_group), pl.ds(t * width, width)]
                    pieces.append(lax.dot_general(
                        w, place[g], (((0,), (0,)), ((), ())), preferred_element_type=f32
                    ).astype(bf16))
                wp = jnp.concatenate(pieces, axis=0)
                col = (k * gph + m * pair) * width
                part = jnp.dot(picked[t][:, col : col + 128], wp, preferred_element_type=f32)
                acc = part if acc is None else acc + part
        if parts == "q":
            outs[0][k] = normalize(acc[:, :hd]).astype(bf16)
        else:
            outs[0][0, 0, k] = normalize(acc[:, :hd]).T.astype(bf16)
            outs[0][1, 0, k] = acc[:, hd:].astype(bf16)


def post_kernel(idx_ref, sharp_ref, q_ref, kv_ref, wup_ref, res_ref, oct_ref, out_ref, att_scr):
    me = idx_ref[0]
    heads, tq, hd = q_ref.shape
    f32, bf16 = jnp.float32, jnp.bfloat16
    nb = kv_ref.shape[1]
    qpos = me * tq + lax.broadcasted_iota(jnp.int32, (tq, nb * tq), 0)
    kpos = lax.broadcasted_iota(jnp.int32, (tq, nb * tq), 1)
    visible = kpos <= qpos
    for h in range(heads):
        q = q_ref[h]
        sharp = sharp_ref[h]
        keys_t = jnp.concatenate([kv_ref[0, d, h] for d in range(nb)], axis=1)
        vals = jnp.concatenate([kv_ref[1, d, h] for d in range(nb)], axis=0)
        s = jnp.dot(q, keys_t, preferred_element_type=f32) * sharp
        w = jnp.where(visible, jnp.exp(s - sharp), jnp.zeros((), f32))
        den = jnp.sum(w, axis=1, keepdims=True)
        num = jnp.dot(w.astype(bf16), vals, preferred_element_type=f32)
        att_scr[:, h * hd : (h + 1) * hd] = (num / den).astype(bf16)

    rows, width = res_ref.shape
    row_blocks = rows // 128
    tok_blk = 128 // SHORTEN
    n_chunks = wup_ref.shape[0]
    cin = wup_ref.shape[1] // SHORTEN
    cout = wup_ref.shape[2]
    r_i = lax.broadcasted_iota(jnp.int32, (128, tok_blk), 0)
    j_i = lax.broadcasted_iota(jnp.int32, (128, tok_blk), 1)
    for rb in range(row_blocks):
        a_blk = att_scr[pl.ds(rb * tok_blk, tok_blk), :]
        expanded = []
        for t in range(SHORTEN):
            sel = (r_i == SHORTEN * j_i + t).astype(bf16)
            expanded.append(jnp.dot(sel, a_blk, preferred_element_type=f32).astype(bf16))
        hid = []
        ss = jnp.zeros((128, 1), f32)
        for k in range(n_chunks):
            lhs = jnp.concatenate([expanded[t][:, k * cin : (k + 1) * cin] for t in range(SHORTEN)], axis=1)
            u = jnp.dot(lhs, wup_ref[k], preferred_element_type=f32)
            hcol = res_ref[pl.ds(rb * 128, 128), pl.ds(k * cout, cout)].astype(f32) + u
            hid.append(hcol)
            ss = ss + jnp.sum(hcol * hcol, axis=1, keepdims=True)
        scale = lax.rsqrt(ss / width + 1e-05)
        acc = None
        for k in range(n_chunks):
            part = jnp.dot(
                (hid[k] * scale).astype(bf16),
                oct_ref[pl.ds(k * cout, cout), :],
                preferred_element_type=f32,
            )
            acc = part if acc is None else acc + part
        out_ref[pl.ds(rb * 128, 128), :] = (acc * width ** (-0.5)).astype(out_ref.dtype)


def on_device(
    residual_stream, octet_readout, downsampling_filter, sharpness_factor, widening_filter
):
    byte_rows = residual_stream.shape[0]
    groups = downsampling_filter.shape[0]
    per_group = downsampling_filter.shape[2] // 3
    attention_number = sharpness_factor.shape[0]
    head_size = groups * per_group // attention_number
    tokens_here = byte_rows // SHORTEN
    rim_rows = SHORTEN - 1
    left_rim = shifted_2(residual_stream[byte_rows - rim_rows :], "seq", 1)
    vmem = pl.BlockSpec(memory_space=pltpu.VMEM)
    smem = pl.BlockSpec(memory_space=pltpu.SMEM)
    params = pltpu.CompilerParams(vmem_limit_bytes=60 * 1024 * 1024)
    filter_t = jnp.swapaxes(downsampling_filter, 1, 2)
    stacked = pl.pallas_call(
        functools.partial(shorten_kernel, parts="kv"),
        out_shape=jax.ShapeDtypeStruct((2, 1, attention_number, tokens_here, head_size), jnp.bfloat16),
        in_specs=[vmem, vmem, vmem],
        out_specs=vmem,
        compiler_params=params,
    )(residual_stream, left_rim, filter_t)
    gathered = lax.all_gather(stacked, "seq", axis=1, tiled=True)
    queries = pl.pallas_call(
        functools.partial(shorten_kernel, parts="q"),
        out_shape=jax.ShapeDtypeStruct((attention_number, tokens_here, head_size), jnp.bfloat16),
        in_specs=[vmem, vmem, vmem],
        out_specs=vmem,
        compiler_params=params,
    )(residual_stream, left_rim, filter_t)
    my_index = lax.axis_index("seq").astype(jnp.int32).reshape(1)
    wup = widening_blocks(widening_filter, attention_number)
    return pl.pallas_call(
        post_kernel,
        out_shape=jax.ShapeDtypeStruct((byte_rows, octet_readout.shape[0]), jnp.bfloat16),
        in_specs=[smem, smem, vmem, vmem, vmem, vmem, vmem],
        out_specs=vmem,
        scratch_shapes=[pltpu.VMEM((tokens_here, attention_number * head_size), jnp.bfloat16)],
        compiler_params=pltpu.CompilerParams(vmem_limit_bytes=60 * 1024 * 1024),
    )(my_index, sharpness_factor, queries, gathered, wup, residual_stream, octet_readout.T)


def solution(mesh):
    in_specs = (P(("dp", "seq"), None), P(), P(), P(), P())
    out_specs = P(("dp", "seq"), None)
    return jax.shard_map(
        on_device, mesh=mesh, in_specs=in_specs, out_specs=out_specs, check_vma=False
    )
```

```python
import functools

import jax
import jax.numpy as jnp
from jax import lax
from jax.experimental import pallas as pl
from jax.experimental.pallas import tpu as pltpu
from jax.sharding import PartitionSpec as P

SHORTEN = 4


def shifted_2(array, axis, by):
    count = lax.axis_size(axis)
    pairs = [(i, i + by) for i in range(count) if 0 <= i + by < count]
    return lax.ppermute(array, axis, pairs)


def normalize(vectors):
    return vectors * lax.rsqrt(jnp.sum(vectors * vectors, axis=-1, keepdims=True) + 1e-06)


def widening_blocks(widening_filter, heads):
    groups, per_group, span = widening_filter.shape
    gph = groups // heads
    width = span // SHORTEN
    wf = widening_filter.reshape(heads, gph, per_group, SHORTEN, width)
    wf = wf.transpose(3, 0, 1, 2, 4)[:, :, :, :, None, :]
    eye = jnp.eye(gph, dtype=jnp.bool_)[:, None, :, None]
    blocks = jnp.where(eye, wf, jnp.zeros((), wf.dtype))
    blocks = blocks.reshape(SHORTEN, heads, gph * per_group, gph * width).transpose(1, 0, 2, 3)
    return blocks.reshape(heads, SHORTEN * gph * per_group, gph * width)


def shorten_kernel(res_ref, rim_ref, wd_ref, *outs, parts):
    f32, bf16 = jnp.float32, jnp.bfloat16
    rows = res_ref.shape[0]
    tokens = rows // SHORTEN
    heads = outs[0].shape[-3]
    hd = outs[0].shape[-1]
    groups, channels, span = wd_ref.shape
    gph = groups // heads
    width = span // SHORTEN
    per_group = channels // 3
    j_i = lax.broadcasted_iota(jnp.int32, (tokens, rows), 0)
    r_i = lax.broadcasted_iota(jnp.int32, (tokens, rows), 1)
    first = lax.broadcasted_iota(jnp.int32, (tokens, 1), 0) == 0
    res = res_ref[...]
    picked = []
    for t in range(SHORTEN):
        sel = (r_i == SHORTEN * j_i + t - (SHORTEN - 1)).astype(bf16)
        x = jnp.dot(sel, res, preferred_element_type=f32).astype(bf16)
        if t < SHORTEN - 1:
            x = jnp.where(first, rim_ref[pl.ds(t, 1), :], x)
        picked.append(x)
    first_part = 0 if parts == "q" else 1
    n_parts = 1 if parts == "q" else 2
    i_i = lax.broadcasted_iota(jnp.int32, (n_parts * per_group, n_parts * hd), 0)
    n_i = lax.broadcasted_iota(jnp.int32, (n_parts * per_group, n_parts * hd), 1)
    place = [
        (n_i == (i_i // per_group) * hd + g * per_group + i_i % per_group).astype(bf16)
        for g in range(gph)
    ]
    pair = 128 // width
    for k in range(heads):
        acc = None
        for m in range(gph // pair):
            for t in range(SHORTEN):
                pieces = []
                for e in range(pair):
                    g = m * pair + e
                    w = wd_ref[k * gph + g, pl.ds(first_part * per_group, n_parts * per_group), pl.ds(t * width, width)]
                    pieces.append(lax.dot_general(
                        w, place[g], (((0,), (0,)), ((), ())), preferred_element_type=f32
                    ).astype(bf16))
                wp = jnp.concatenate(pieces, axis=0)
                col = (k * gph + m * pair) * width
                part = jnp.dot(picked[t][:, col : col + 128], wp, preferred_element_type=f32)
                acc = part if acc is None else acc + part
        if parts == "q":
            outs[0][k] = normalize(acc[:, :hd]).astype(bf16)
        else:
            outs[0][0, 0, k] = normalize(acc[:, :hd]).T.astype(bf16)
            outs[0][1, 0, k] = acc[:, hd:].astype(bf16)


def post_kernel(idx_ref, sharp_ref, q_ref, kv_ref, wup_ref, res_ref, oct_ref, out_ref, att_scr):
    me = idx_ref[0]
    heads, tq, hd = q_ref.shape
    f32, bf16 = jnp.float32, jnp.bfloat16
    nb = kv_ref.shape[1]
    qpos = me * tq + lax.broadcasted_iota(jnp.int32, (tq, nb * tq), 0)
    kpos = lax.broadcasted_iota(jnp.int32, (tq, nb * tq), 1)
    visible = kpos <= qpos
    for h in range(heads):
        q = q_ref[h]
        sharp = sharp_ref[h]
        keys_t = jnp.concatenate([kv_ref[0, d, h] for d in range(nb)], axis=1)
        s = jnp.dot(q, keys_t, preferred_element_type=f32) * sharp
        w = jnp.where(visible, jnp.exp(s - sharp), jnp.zeros((), f32))
        den = jnp.sum(w, axis=1, keepdims=True)
        w_low = w.astype(bf16)
        num = jnp.dot(w_low[:, :tq], kv_ref[1, 0, h], preferred_element_type=f32)
        for d in range(1, nb):
            num = num + jnp.dot(w_low[:, d * tq : (d + 1) * tq], kv_ref[1, d, h], preferred_element_type=f32)
        att_scr[:, h * hd : (h + 1) * hd] = (num / den).astype(bf16)

    rows, width = res_ref.shape
    row_blocks = rows // 128
    tok_blk = 128 // SHORTEN
    n_chunks = wup_ref.shape[0]
    cin = wup_ref.shape[1] // SHORTEN
    cout = wup_ref.shape[2]
    r_i = lax.broadcasted_iota(jnp.int32, (128, tok_blk), 0)
    j_i = lax.broadcasted_iota(jnp.int32, (128, tok_blk), 1)
    for rb in range(row_blocks):
        a_blk = att_scr[pl.ds(rb * tok_blk, tok_blk), :]
        expanded = []
        for t in range(SHORTEN):
            sel = (r_i == SHORTEN * j_i + t).astype(bf16)
            expanded.append(jnp.dot(sel, a_blk, preferred_element_type=f32).astype(bf16))
        hid = []
        ss = jnp.zeros((128, 1), f32)
        for k in range(n_chunks):
            lhs = jnp.concatenate([expanded[t][:, k * cin : (k + 1) * cin] for t in range(SHORTEN)], axis=1)
            u = jnp.dot(lhs, wup_ref[k], preferred_element_type=f32)
            hcol = res_ref[pl.ds(rb * 128, 128), pl.ds(k * cout, cout)].astype(f32) + u
            hid.append(hcol)
            ss = ss + jnp.sum(hcol * hcol, axis=1, keepdims=True)
        scale = lax.rsqrt(ss / width + 1e-05)
        acc = None
        for k in range(n_chunks):
            part = jnp.dot(
                (hid[k] * scale).astype(bf16),
                oct_ref[pl.ds(k * cout, cout), :],
                preferred_element_type=f32,
            )
            acc = part if acc is None else acc + part
        out_ref[pl.ds(rb * 128, 128), :] = (acc * width ** (-0.5)).astype(out_ref.dtype)


def on_device(
    residual_stream, octet_readout, downsampling_filter, sharpness_factor, widening_filter
):
    byte_rows = residual_stream.shape[0]
    groups = downsampling_filter.shape[0]
    per_group = downsampling_filter.shape[2] // 3
    attention_number = sharpness_factor.shape[0]
    head_size = groups * per_group // attention_number
    tokens_here = byte_rows // SHORTEN
    rim_rows = SHORTEN - 1
    left_rim = shifted_2(residual_stream[byte_rows - rim_rows :], "seq", 1)
    vmem = pl.BlockSpec(memory_space=pltpu.VMEM)
    smem = pl.BlockSpec(memory_space=pltpu.SMEM)
    params = pltpu.CompilerParams(vmem_limit_bytes=60 * 1024 * 1024)
    filter_t = jnp.swapaxes(downsampling_filter, 1, 2)
    stacked = pl.pallas_call(
        functools.partial(shorten_kernel, parts="kv"),
        out_shape=jax.ShapeDtypeStruct((2, 1, attention_number, tokens_here, head_size), jnp.bfloat16),
        in_specs=[vmem, vmem, vmem],
        out_specs=vmem,
        compiler_params=params,
    )(residual_stream, left_rim, filter_t)
    gathered = lax.all_gather(stacked, "seq", axis=1, tiled=True)
    queries = pl.pallas_call(
        functools.partial(shorten_kernel, parts="q"),
        out_shape=jax.ShapeDtypeStruct((attention_number, tokens_here, head_size), jnp.bfloat16),
        in_specs=[vmem, vmem, vmem],
        out_specs=vmem,
        compiler_params=params,
    )(residual_stream, left_rim, filter_t)
    my_index = lax.axis_index("seq").astype(jnp.int32).reshape(1)
    wup = widening_blocks(widening_filter, attention_number)
    return pl.pallas_call(
        post_kernel,
        out_shape=jax.ShapeDtypeStruct((byte_rows, octet_readout.shape[0]), jnp.bfloat16),
        in_specs=[smem, smem, vmem, vmem, vmem, vmem, vmem],
        out_specs=vmem,
        scratch_shapes=[pltpu.VMEM((tokens_here, attention_number * head_size), jnp.bfloat16)],
        compiler_params=pltpu.CompilerParams(vmem_limit_bytes=60 * 1024 * 1024),
    )(my_index, sharpness_factor, queries, gathered, wup, residual_stream, octet_readout.T)


def solution(mesh):
    in_specs = (P(("dp", "seq"), None), P(), P(), P(), P())
    out_specs = P(("dp", "seq"), None)
    return jax.shard_map(
        on_device, mesh=mesh, in_specs=in_specs, out_specs=out_specs, check_vma=False
    )
```
